32 devices in a mesh: replica: 2 (over x), fsdp: 4 (over y, core), ctx: 4 (over z).
Axes of the slice: x: 2, y: 2, z: 4, core: 2. Of those that a mesh axis runs over, the one named last changes fastest.
Arguments:
- hidden_in: bfloat16 [8, 1024, 2048], P(('replica', 'fsdp'), 'ctx'), may hold values from -6 to 6
- teacher: bfloat16 [8, 1024, 2048], P(('replica', 'fsdp'), 'ctx'), may hold values from -6 to 6
- valid_mask: int32 [8, 1024], P(('replica', 'fsdp'), 'ctx'), may hold values from 0 to 1, as said below
- layout: int32 [8, 1024], P(('replica', 'fsdp')), may hold values from 0 to 7, never falling along the last dimension, each value on 1 to 256 neighbouring positions
- routes: int32 [8, 1024, 2], P(('replica', 'fsdp'), 'ctx'), may hold values from 0 to 15, all different within a row; in each aligned block of 256 rows (0 to 255, 256 to 511, ..., all dimensions but the last counted through in order) at most 40 rows name the same one
- attn_gain: bfloat16 [2048], P('fsdp'), may hold values from 0.5 to 1.5
- w_query: bfloat16 [2048, 3072], P('fsdp'), may hold values from -0.125 to 0.125
- w_latent: bfloat16 [2048, 576], P('fsdp'), may hold values from -0.125 to 0.125
- latent_gain: bfloat16 [512], P('fsdp'), may hold values from 0.5 to 1.5
- w_expand: bfloat16 [512, 4096], P('fsdp'), may hold values from -0.25 to 0.25
- w_out: bfloat16 [2048, 2048], P('fsdp'), may hold values from -1.5 to 1.5
- ffn_gain: bfloat16 [2048], P('fsdp'), may hold values from 0.5 to 1.5
- w_router: bfloat16 [2048, 16], P('fsdp'), may hold values from -0.09375 to 0.09375
- shared_gate: bfloat16 [2048, 2816], P('fsdp'), may hold values from -0.125 to 0.125
- shared_up: bfloat16 [2048, 2816], P('fsdp'), may hold values from -0.125 to 0.125
- shared_down: bfloat16 [2816, 2048], P('fsdp'), may hold values from -0.15625 to 0.15625
- expert_gate: bfloat16 [16, 2048, 1408], P(('fsdp', 'ctx'), None, 'replica'), may hold values from -0.125 to 0.125
- expert_up: bfloat16 [16, 2048, 1408], P(('fsdp', 'ctx'), None, 'replica'), may hold values from -0.125 to 0.125
- expert_down: bfloat16 [16, 1408, 2048], P(('fsdp', 'ctx'), 'replica'), may hold values from -0.3125 to 0.3125
Outputs:
- output: bfloat16 [8, 1024, 2048], P(('replica', 'fsdp'), 'ctx')
- loss_value: float32 [], replicated
- input_grad: float32 [8, 1024, 2048], P(('replica', 'fsdp'), 'ctx')
- attn_gain_grad: float32 [2048], P('fsdp')
- w_query_grad: float32 [2048, 3072], P('fsdp')
- w_latent_grad: float32 [2048, 576], P('fsdp')
- latent_gain_grad: float32 [512], P('fsdp')
- w_expand_grad: float32 [512, 4096], P('fsdp')
- w_out_grad: float32 [2048, 2048], P('fsdp')
- ffn_gain_grad: float32 [2048], P('fsdp')
- w_router_grad: float32 [2048, 16], P('fsdp')
- shared_gate_grad: float32 [2048, 2816], P('fsdp')
- shared_up_grad: float32 [2048, 2816], P('fsdp')
- shared_down_grad: float32 [2816, 2048], P('fsdp')
- expert_gate_grad: float32 [16, 2048, 1408], P(('fsdp', 'ctx'), None, 'replica')
- expert_up_grad: float32 [16, 2048, 1408], P(('fsdp', 'ctx'), None, 'replica')
- expert_down_grad: float32 [16, 1408, 2048], P(('fsdp', 'ctx'), 'replica')
The draws below stay inside these ranges and needn't reach their ends.
Inputs may be any that keep to these rules, and one draw needn't show every extreme that they name: `routes`: each row names 2 different experts; within the rows of one device (aligned blocks of 256 rows) no expert is named more than 40 times. `layout`: within each sequence block numbers start at 0, never fall, and each block holds 1 to 256 positions. `valid_mask`: the first position of every sequence is valid.
All inputs are finite; a program needn't handle non-finite values.
Results may differ from the reference program's by a relative error of at most 0.02.
Values may be sent and summed in bfloat16 or wider, within the bound.
A program may use at most 448 MiB of HBM per device.

```python
import math
import jax
import jax.numpy as jnp
import numpy as np
from jax import lax

D = 2048
HEADS = 16
NOPE = 128
ROPE = 64
VDIM = 128
LATENT = 512
MOE_FF = 1408
SHARED_FF = 2816
TOP = 2
BLOCK = 256
TOK_DEV = 256
EXPERTS = 16
LEN = 1024
SEQS = 8
SEGS = 8
CAP = 40
N_REPLICA = 2


def draw_valid_mask(key, part):
    positions = jnp.arange(LEN, dtype=jnp.int32)[None, :]
    sequence = jnp.arange(SEQS, dtype=jnp.int32)[:, None]
    level = (950 - 650 * positions // LEN) * (400 + 600 * sequence // SEQS) // 1000
    drawn = jax.random.randint(key, (SEQS, LEN), 0, 1000, dtype=jnp.int32)
    return jnp.where((drawn < level) | (positions == 0), 1, 0).astype(jnp.int32)


def steps_of(key, shape, split, least, high):
    factor_of = 1.0
    for axis_at, blocks in split:
        steps = jax.random.uniform(jax.random.fold_in(jax.random.fold_in(key, 6), axis_at), (blocks,), jnp.float32, least / len(split), high / len(split))
        factor_of = factor_of * jnp.repeat(jnp.exp(steps), shape[axis_at] // blocks).reshape((-1,) + (1,) * (len(shape) - 1 - axis_at))
    return factor_of


def profile(number_of, total, limit, skew):
    loads = [(1 << 20) // math.isqrt(standing ** skew) + 1 for standing in range(2, number_of + 1)]
    spare, holding = total - limit - (number_of - 1), [1] * (number_of - 1)
    while spare > 0:
        candidates = [i for i in range(number_of - 1) if holding[i] < limit]
        mass, remaining = sum([loads[i] for i in candidates]), spare
        for i in candidates:
            more = min(limit - holding[i], max(1, remaining * loads[i] // mass), spare)
            holding[i] = holding[i] + more
            spare = spare - more
    return np.array([limit] + holding)


def uneven_parts(rng, number_of, total, most, skew):
    if number_of == 2:
        one = jax.random.randint(rng, (), max(1, total - most), min(most, total - 1) + 1)
        return jnp.stack([one, total - one])
    sizes = jnp.asarray(profile(number_of, total, most, skew), jnp.int32)
    couples = (number_of - 1) // 2
    donor, sink = sizes[1:1 + 2 * couples:2], sizes[2:2 + 2 * couples:2]
    slack = jnp.minimum(donor - 1, most - sink)
    moved = jax.random.randint(jax.random.fold_in(rng, 1), (couples,), 0, 1 << 20) % (slack + 1)
    sizes = sizes.at[1:1 + 2 * couples:2].set(donor - moved).at[2:2 + 2 * couples:2].set(sink + moved)
    return sizes[jax.random.permutation(jax.random.fold_in(rng, 2), number_of)]


def deal_out(own_key, own, number, rows, number_of, top, most, lean):
    order = jax.random.permutation(own_key, number_of)
    packed, ordinary = portions_of(number_of, rows * top, most, lean, True), portions_of(number_of, rows * top, most, lean, False)
    places = jnp.arange(number_of)

    def named(lengths, rotation):
        used = int((lengths > 0).sum())
        fixed = max(1, used // 4)
        moved = fixed + (places - fixed + rotation * (used - fixed)) % max(1, number_of - fixed)
        return jnp.zeros((number_of,), jnp.int32).at[order[jnp.where(places < fixed, places, moved)]].set(jnp.asarray(lengths, jnp.int32))

    lengths = jnp.where(number % 4 == 0, named(packed, number // 4), named(ordinary, number - number // 4 - 1))
    mixed = jax.random.permutation(jax.random.fold_in(own, 3), number_of)
    donor, taker = mixed[0:number_of // 2 * 2:2], mixed[1:number_of // 2 * 2:2]
    room = jnp.minimum(lengths[donor] - 1, most - lengths[taker]) // 2
    room = jnp.where((donor == order[0]) | (taker == order[0]) | (lengths[taker] == 0), 0, jnp.maximum(room, 0))
    moved = jax.random.randint(jax.random.fold_in(own, 4), (number_of // 2,), 0, 1 << 20) % (room + 1)
    lengths = lengths.at[donor].add(-moved).at[taker].add(moved)
    items = jnp.searchsorted(jnp.cumsum(lengths), jnp.arange(rows * top), side="right").astype(jnp.int32)
    grid = items.reshape(top, rows).T
    grid = grid[jax.random.permutation(jax.random.fold_in(own, 1), rows)]
    rotation = jax.random.randint(jax.random.fold_in(own, 2), (rows, 1), 0, top)
    return jnp.take_along_axis(grid, (jnp.arange(top)[None, :] + rotation) % top, axis=1)


def portions_of(number_of, total, most, lean, full):
    weights = [(1 << 20) // math.isqrt(standing ** lean) + 1 for standing in range(1, number_of + 1)]
    largest = most if full else min(most, max(-(-total // number_of), total * weights[0] // sum(weights)))
    least = 1 if total - largest >= number_of - 1 else 0
    holding, rest = [largest] + [least] * (number_of - 1), total - largest - least * (number_of - 1)
    while rest > 0:
        movable = [i for i in range(1, number_of) if holding[i] < largest] or [i for i in range(1, number_of) if holding[i] < most]
        whole, left = sum([weights[i] for i in movable]), rest
        for i in movable:
            more = min(most - holding[i], max(1, left * weights[i] // whole), rest)
            holding[i] = holding[i] + more
            rest = rest - more
    return np.array(holding)


def centred(key, shape, deviation, bound, cuts=(), kind=jnp.bfloat16):
    array = jax.random.normal(key, shape, jnp.float32) * deviation
    if len(cuts) > 0:
        array = steps_of(key, shape, cuts, -0.22, 0.18) * array
    return jnp.clip(array, min=-bound, max=bound).astype(kind)


def setup_inputs(seed: int = 0) -> dict:
    seeds = jax.random.split(jax.random.key(seed), 20)
    hidden_in = centred(seeds[0], (SEQS, LEN, D), 1.0, 6.0, ((0, 8), (1, 4)))
    teacher = centred(seeds[1], (SEQS, LEN, D), 1.0, 6.0, ((0, 8), (1, 4)))
    valid_mask = draw_valid_mask(jax.random.fold_in(seeds[19], 71), 0)
    layout = jax.vmap(lambda own: jnp.searchsorted(jnp.cumsum(uneven_parts(own, SEGS, LEN, BLOCK, 0)), jnp.arange(LEN), side="right"))(jax.random.split(seeds[3], SEQS)).reshape((SEQS, LEN)).astype(jnp.int32)
    routes_keys = jax.random.split(jax.random.fold_in(seeds[4], 1), SEQS * LEN // TOK_DEV)
    routes_turns = jax.random.permutation(jax.random.fold_in(seeds[4], 3), SEQS * LEN // TOK_DEV)
    routes = jax.vmap(lambda own, number: deal_out(jax.random.fold_in(seeds[4], 2), own, number, TOK_DEV, EXPERTS, TOP, CAP, 1))(routes_keys, routes_turns).reshape((SEQS, LEN, TOP))
    attn_gain = jnp.clip(1.0 + 0.1 * jax.random.normal(seeds[5], (D,), jnp.float32), 0.5, 1.5).astype(jnp.bfloat16)
    w_query = centred(seeds[6], (D, HEADS * (NOPE + ROPE)), D ** -0.5, 0.125, ((0, 4),))
    w_latent = centred(seeds[7], (D, LATENT + ROPE), D ** -0.5, 0.125, ((0, 4),))
    latent_gain = jnp.clip(1.0 + 0.1 * jax.random.normal(seeds[8], (LATENT,), jnp.float32), 0.5, 1.5).astype(jnp.bfloat16)
    w_expand = centred(seeds[9], (LATENT, HEADS * (NOPE + VDIM)), LATENT ** -0.5, 0.25, ((0, 4),))
    w_out = centred(seeds[10], (HEADS * VDIM, D), 16 ** -0.5, 1.5, ((0, 4),))
    ffn_gain = jnp.clip(1.0 + 0.1 * jax.random.normal(seeds[11], (D,), jnp.float32), 0.5, 1.5).astype(jnp.bfloat16)
    w_router = centred(seeds[12], (D, EXPERTS), (2 * D) ** -0.5, 0.09375, ((0, 4),))
    shared_gate = centred(seeds[13], (D, SHARED_FF), D ** -0.5, 0.125, ((0, 4),))
    shared_up = centred(seeds[14], (D, SHARED_FF), D ** -0.5, 0.125, ((0, 4),))
    shared_down = centred(seeds[15], (SHARED_FF, D), (SHARED_FF // 2) ** -0.5, 0.15625, ((0, 4),))
    expert_gate = centred(seeds[16], (EXPERTS, D, MOE_FF), D ** -0.5, 0.125, ((0, 16), (2, 2)))
    expert_up = centred(seeds[17], (EXPERTS, D, MOE_FF), D ** -0.5, 0.125, ((0, 16), (2, 2)))
    expert_down = centred(seeds[18], (EXPERTS, MOE_FF, D), (MOE_FF // 4) ** -0.5, 0.3125, ((0, 16), (1, 2)))
    return {"hidden_in": hidden_in, "teacher": teacher, "valid_mask": valid_mask, "layout": layout, "routes": routes, "attn_gain": attn_gain, "w_query": w_query, "w_latent": w_latent, "latent_gain": latent_gain, "w_expand": w_expand, "w_out": w_out, "ffn_gain": ffn_gain, "w_router": w_router, "shared_gate": shared_gate, "shared_up": shared_up, "shared_down": shared_down, "expert_gate": expert_gate, "expert_up": expert_up, "expert_down": expert_down}


HIGHEST = lax.Precision.HIGHEST

@jax.custom_vjp
def low(v):
    return lax.optimization_barrier(v.astype(jnp.bfloat16)).astype(jnp.float32)

@jax.custom_vjp
def low_back(v):
    return v

def low_keep(v):
    return (low(v), None)

def low_pass(kept, grad):
    return (grad,)

def back_keep(v):
    return (v, None)

def back_low(kept, grad):
    return (low(grad),)
low.defvjp(low_keep, low_pass)
low_back.defvjp(back_keep, back_low)

def round_both(values):
    return low(low_back(values))

def matmul(first_mat, second_mat):
    return jnp.dot(first_mat, second_mat, precision=HIGHEST)

def rms_norm(values, gain_vec):
    return values * lax.rsqrt(lax.optimization_barrier(jnp.mean(values * values, axis=-1, keepdims=True)) + 1e-06) * gain_vec

def rotate(values, cosine, sine_part):
    half_width = values.shape[-1] // 2
    first_half = values[..., :half_width]
    second = values[..., half_width:]
    return jnp.concatenate([first_half * cosine - second * sine_part, first_half * sine_part + second * cosine], axis=-1)

def angles():
    positions = jnp.arange(LEN, dtype=jnp.float32)
    inverse = 10000.0 ** (-jnp.arange(ROPE // 2, dtype=jnp.float32) * (2.0 / ROPE))
    phase = positions[:, None] * inverse[None, :]
    return (jnp.cos(phase), jnp.sin(phase))

def attend_one(pieces):
    query, expanded, rope_key, blocks = pieces
    keys_all = jnp.concatenate([expanded[..., :NOPE], jnp.broadcast_to(rope_key[:, None, :], (LEN, HEADS, ROPE))], axis=-1)
    value_rows = expanded[..., NOPE:]
    scores = low_back(jnp.einsum('qhd,khd->hqk', query, keys_all, precision=HIGHEST) * (NOPE + ROPE) ** (-0.5))
    allowed = blocks[None, :] <= blocks[:, None]
    scores = jnp.where(allowed[None], scores, -1e+30)
    attn_probs = low(jax.nn.softmax(scores, axis=-1))
    return jnp.einsum('hqk,khv->qhv', attn_probs, value_rows, precision=HIGHEST)

def routed_experts(normed_two, chosen_ids, expert_gate, expert_up, expert_down):
    token_count = normed_two.shape[0]
    block_count = token_count // TOK_DEV
    block_ids = chosen_ids.reshape(block_count, TOK_DEV * TOP)
    hits = (block_ids[..., None] == jnp.arange(EXPERTS, dtype=jnp.int32)[None, None, :]).astype(jnp.int32)
    ranks = lax.optimization_barrier(jnp.sum((jnp.cumsum(hits, axis=1) - hits) * hits, axis=-1))
    slots = block_ids * CAP + ranks

    def owners(slot_row):
        return jnp.full((EXPERTS * CAP,), TOK_DEV, jnp.int32).at[slot_row].set(jnp.arange(TOK_DEV * TOP, dtype=jnp.int32) // TOP)
    owner = jax.vmap(owners)(slots)
    blocks = normed_two.reshape(block_count, TOK_DEV, D)
    padded = jnp.concatenate([blocks, jnp.zeros((block_count, 1, D), normed_two.dtype)], axis=1)
    buffer = jax.vmap(lambda block_rows, owner_row: jnp.take(block_rows, owner_row, axis=0))(padded, owner)
    buffer = buffer.reshape(block_count, EXPERTS, CAP, D).transpose(1, 0, 2, 3).reshape(EXPERTS, block_count * CAP, D)
    half_width = MOE_FF // N_REPLICA
    summed = jnp.zeros((EXPERTS, block_count * CAP, D), normed_two.dtype)
    for part_index in range(N_REPLICA):
        lower = part_index * half_width
        upper = lower + half_width
        part_rows = low_back(buffer)
        gate_in = low_back(jnp.einsum('erd,edf->erf', part_rows, expert_gate[:, :, lower:upper], precision=HIGHEST))
        up_in = low_back(jnp.einsum('erd,edf->erf', part_rows, expert_up[:, :, lower:upper], precision=HIGHEST))
        act_rows = low(jax.nn.silu(gate_in) * up_in)
        summed = summed + low(jnp.einsum('erf,efd->erd', act_rows, expert_down[:, lower:upper, :], precision=HIGHEST))
    expert_rows = low_back(summed)
    expert_rows = expert_rows.reshape(EXPERTS, block_count, CAP, D).transpose(1, 0, 2, 3).reshape(block_count, EXPERTS * CAP, D)
    picked = jax.vmap(lambda block_rows, slot_row: jnp.take(block_rows, slot_row, axis=0))(expert_rows, slots)
    return picked.reshape(token_count, TOP, D)

def layer_forward(weights, hidden, target, valid_rows, blocks, route_ids):
    gain_one, w_query, w_latent, gain_latent, w_expand, w_out, gain_two, w_router, shared_gate, shared_up, shared_down, expert_gate, expert_up, expert_down = weights
    seq_count = hidden.shape[0]
    token_rows = hidden.reshape(seq_count * LEN, D)
    cosine, sine_part = angles()
    normed = low(rms_norm(token_rows, gain_one))
    query_raw = low_back(matmul(normed, w_query)).reshape(seq_count, LEN, HEADS, NOPE + ROPE)
    query = low(jnp.concatenate([query_raw[..., :NOPE], rotate(query_raw[..., NOPE:], cosine[None, :, None, :], sine_part[None, :, None, :])], axis=-1))
    latent_raw = low_back(matmul(normed, w_latent)).reshape(seq_count, LEN, LATENT + ROPE)
    latent = low(rms_norm(latent_raw[..., :LATENT], gain_latent))
    rope_key = low(rotate(latent_raw[..., LATENT:], cosine[None], sine_part[None]))
    expanded = round_both(matmul(latent.reshape(seq_count * LEN, LATENT), w_expand)).reshape(seq_count, LEN, HEADS, NOPE + VDIM)
    attended = lax.map(jax.checkpoint(attend_one), (query, expanded, rope_key, blocks))
    attended = round_both(attended.reshape(seq_count * LEN, HEADS * VDIM))
    mixed = token_rows + low_back(matmul(attended, w_out))
    normed_two = low(rms_norm(mixed, gain_two))
    logits = low_back(matmul(normed_two, w_router))
    chosen_ids = route_ids.reshape(seq_count * LEN, TOP)
    gates = jax.nn.softmax(jnp.take_along_axis(logits, chosen_ids, axis=1), axis=-1)
    shared_act = low(jax.nn.silu(low_back(matmul(normed_two, shared_gate))) * low_back(matmul(normed_two, shared_up)))
    shared_out = low_back(matmul(shared_act, shared_down))
    picked = routed_experts(normed_two, chosen_ids, expert_gate, expert_up, expert_down)
    final = mixed + shared_out + lax.optimization_barrier(jnp.sum(gates[:, :, None] * picked, axis=1))
    error_rows = final - target.reshape(seq_count * LEN, D)
    partial_sum = jnp.sum(valid_rows.reshape(seq_count * LEN)[:, None] * error_rows * error_rows)
    return (final.reshape(seq_count, LEN, D), partial_sum)

def reference(hidden_in, teacher, valid_mask, layout, routes, attn_gain, w_query, w_latent, latent_gain, w_expand, w_out, ffn_gain, w_router, shared_gate, shared_up, shared_down, expert_gate, expert_up, expert_down):
    weights = tuple((matrix.astype(jnp.float32) for matrix in (attn_gain, w_query, w_latent, latent_gain, w_expand, w_out, ffn_gain, w_router, shared_gate, shared_up, shared_down, expert_gate, expert_up, expert_down)))
    group_size = max(1, min(SEQS, 4096 // LEN))
    while SEQS % group_size:
        group_size = group_size - 1
    group_count = SEQS // group_size
    target = teacher.astype(jnp.float32).reshape(group_count, group_size, LEN, D)
    valid_rows = valid_mask.astype(jnp.float32).reshape(group_count, group_size, LEN)
    blocks = layout.reshape(group_count, group_size, LEN)
    route_ids = routes.reshape(group_count, group_size, LEN, TOP)
    valid_count = jnp.sum(valid_mask.astype(jnp.float32))

    def forward(inputs, params):

        def group_step(summed, pieces):
            hidden, target_group, valid_group, block_group, route_group = pieces
            final, partial_sum = layer_forward(params, hidden, target_group, valid_group, block_group, route_group)
            return (summed + partial_sum, final)
        summed, finals = lax.scan(jax.checkpoint(group_step), jnp.zeros((), jnp.float32), (inputs.reshape(group_count, group_size, LEN, D), target, valid_rows, blocks, route_ids))
        return (finals.reshape(SEQS, LEN, D), summed / (valid_count * D))
    inputs = hidden_in.astype(jnp.float32)
    (final, loss_value), pull = jax.vjp(forward, inputs, weights)
    input_grad, grads = pull((jnp.zeros_like(final), jnp.ones_like(loss_value)))
    return (final.astype(jnp.bfloat16), loss_value, input_grad, grads[0], grads[1], grads[2], grads[3], grads[4], grads[5], grads[6], grads[7], grads[8], grads[9], grads[10], grads[11], grads[12], grads[13])
```

```python
import jax
import jax.numpy as jnp
from jax import lax
from jax.sharding import PartitionSpec as P

D = 2048
HEADS = 16
NOPE = 128
ROPE = 64
VDIM = 128
LATENT = 512


def rms_norm(values, gain_vec):
    return values * lax.rsqrt(jnp.mean(values * values, axis=-1, keepdims=True) + 1e-06) * gain_vec


def rotate(values, cosine, sine_part):
    half_width = values.shape[-1] // 2
    first_half = values[..., :half_width]
    second = values[..., half_width:]
    return jnp.concatenate(
        [first_half * cosine - second * sine_part, first_half * sine_part + second * cosine],
        axis=-1,
    )


def rows_dot(first_mat, second_mat):
    return lax.dot_general(
        first_mat, second_mat, (((0,), (0,)), ((), ())), preferred_element_type=jnp.float32
    )


def cols_dot(first_mat, second_mat):
    return lax.dot_general(
        first_mat, second_mat, (((1,), (1,)), ((), ())), preferred_element_type=jnp.float32
    )


def matmul(first_mat, second_mat):
    return jnp.dot(first_mat, second_mat, preferred_element_type=jnp.float32)


def silu_slope(gate_in, sigmoid_in):
    return sigmoid_in * (1.0 + gate_in * (1.0 - sigmoid_in))


def masks(count):
    found = []
    mask = count // 2
    while mask:
        found.append(mask)
        mask //= 2
    return found


def swap(values, axis, mask):
    count = lax.axis_size(axis)
    return lax.ppermute(values, axis, [(i, i ^ mask) for i in range(count)])


def upper(axis, mask):
    return (lax.axis_index(axis) // mask) % 2 == 1


def halves(values, axis, mask, dim):
    size = values.shape[dim] // 2
    low = lax.slice_in_dim(values, 0, size, axis=dim)
    high = lax.slice_in_dim(values, size, 2 * size, axis=dim)
    up = upper(axis, mask)
    return jnp.where(up, low, high), jnp.where(up, high, low)


def join_halves(mine, other, axis, mask):
    up = upper(axis, mask)
    return jnp.concatenate([jnp.where(up, other, mine), jnp.where(up, mine, other)], axis=0)


def gather_tokens(values):
    for mask in masks(lax.axis_size("fsdp")):
        values = jnp.concatenate([values, swap(values, "fsdp", mask)], axis=0)
    return values


def own_columns(values):
    for mask in masks(lax.axis_size("fsdp")):
        send, keep = halves(values, "fsdp", mask, 1)
        values = jnp.concatenate([keep, swap(send, "fsdp", mask)], axis=0)
    return values


def scatter_rows(values, axis):
    for mask in masks(lax.axis_size(axis)):
        send, keep = halves(values, axis, mask, 0)
        values = keep + swap(send.astype(jnp.bfloat16), axis, mask).astype(jnp.float32)
    return values


def sum_rows(values):
    values = scatter_rows(values, "replica")
    ctx_masks = masks(lax.axis_size("ctx"))[::-1]
    for mask in ctx_masks:
        send, keep = halves(values, "ctx", mask, 0)
        values = keep + swap(send.astype(jnp.bfloat16), "ctx", mask).astype(jnp.float32)
    values = values.astype(jnp.bfloat16)
    for mask in ctx_masks[::-1]:
        values = join_halves(values, swap(values, "ctx", mask), "ctx", mask)
    for mask in masks(lax.axis_size("replica"))[::-1]:
        values = join_halves(values, swap(values, "replica", mask), "replica", mask)
    return values.astype(jnp.float32)


def total(values):
    return jnp.sum(lax.all_gather(values, ("replica", "fsdp", "ctx"), axis=0, tiled=True))


def per_device(
    hidden_in,
    teacher,
    valid_mask,
    layout,
    routes,
    attn_gain,
    w_query,
    w_latent,
    latent_gain,
    w_expand,
    w_out,
    ffn_gain,
    w_router,
    shared_gate,
    shared_up,
    shared_down,
    expert_gate,
    expert_up,
    expert_down,
):
    rep_count = lax.axis_size("replica")
    rows_dev = hidden_in.shape[1]
    offset = lax.axis_index("ctx") * rows_dev
    resid = hidden_in.reshape(rows_dev, D).astype(jnp.float32)
    target = teacher.reshape(rows_dev, D).astype(jnp.float32)
    valid_rows = valid_mask.reshape(rows_dev).astype(jnp.float32)
    key_block = layout[0]
    query_block = lax.dynamic_slice_in_dim(key_block, offset, rows_dev)
    route_ids = routes.reshape(rows_dev, routes.shape[-1])
    top_count = route_ids.shape[1]
    gain_one, query_mat, latent_mat, gain_latent, expand_mat, out_mat = (
        lax.all_gather(attn_gain, "fsdp", axis=0, tiled=True),
        lax.all_gather(w_query, "fsdp", axis=0, tiled=True),
        lax.all_gather(w_latent, "fsdp", axis=0, tiled=True),
        lax.all_gather(latent_gain, "fsdp", axis=0, tiled=True),
        lax.all_gather(w_expand, "fsdp", axis=0, tiled=True),
        lax.all_gather(w_out, "fsdp", axis=0, tiled=True),
    )
    valid_count = total(valid_mask).astype(jnp.float32)
    gain_one = gain_one.astype(jnp.float32)
    gain_latent = gain_latent.astype(jnp.float32)
    positions = (offset + jnp.arange(rows_dev)).astype(jnp.float32)
    inverse = 10000.0 ** (-jnp.arange(ROPE // 2, dtype=jnp.float32) * (2.0 / ROPE))
    phase = positions[:, None] * inverse[None, :]
    cosine = jnp.cos(phase)
    sine_part = jnp.sin(phase)

    def turn_query(values):
        return rotate(values, cosine[:, None, :], sine_part[:, None, :])

    def turn_key(values):
        return rotate(values, cosine, sine_part)

    normed = rms_norm(resid, gain_one).astype(jnp.bfloat16)
    query_raw = matmul(normed, query_mat).reshape(rows_dev, HEADS, NOPE + ROPE)
    query_rot = jnp.concatenate(
        [query_raw[..., :NOPE], turn_query(query_raw[..., NOPE:])], axis=-1
    ).astype(jnp.bfloat16)
    latent_raw = matmul(normed, latent_mat)
    latent_part = latent_raw[:, :LATENT]
    rope_part = latent_raw[:, LATENT:]
    latent_own = rms_norm(latent_part, gain_latent).astype(jnp.bfloat16)
    rope_own = turn_key(rope_part).astype(jnp.bfloat16)
    latent_rope = lax.all_gather(
        jnp.concatenate([latent_own, rope_own], axis=1), "ctx", axis=0, tiled=True
    )
    latent_all, rope_all = latent_rope[:, :LATENT], latent_rope[:, LATENT:]
    key_count = latent_all.shape[0]
    expanded = (
        matmul(latent_all, expand_mat).astype(jnp.bfloat16).reshape(key_count, HEADS, NOPE + VDIM)
    )
    key_full = jnp.concatenate(
        [expanded[..., :NOPE], jnp.broadcast_to(rope_all[:, None, :], (key_count, HEADS, ROPE))],
        axis=-1,
    )
    value_rows = expanded[..., NOPE:]
    score_scale = (NOPE + ROPE) ** (-0.5)
    allowed = key_block[None, :] <= query_block[:, None]

    def score_rows():
        raw_scores = (
            jnp.einsum("qhd,khd->hqk", query_rot, key_full, preferred_element_type=jnp.float32)
            * score_scale
        )
        return jnp.where(allowed[None], raw_scores, -1e30)

    scores = score_rows()
    peak = jnp.max(scores, axis=-1, keepdims=True)
    log_total = peak + jnp.log(jnp.sum(jnp.exp(scores - peak), axis=-1, keepdims=True))
    attn_probs = jnp.exp(scores - log_total).astype(jnp.bfloat16)
    attended = (
        jnp.einsum("hqk,khv->qhv", attn_probs, value_rows, preferred_element_type=jnp.float32)
        .reshape(rows_dev, HEADS * VDIM)
        .astype(jnp.bfloat16)
    )
    mixed = resid + matmul(attended, out_mat)
    gain_two, router_mat, share_gate_mat, share_up_mat, share_down_mat = (
        lax.all_gather(ffn_gain, "fsdp", axis=0, tiled=True),
        lax.all_gather(w_router, "fsdp", axis=0, tiled=True),
        lax.all_gather(shared_gate, "fsdp", axis=0, tiled=True),
        lax.all_gather(shared_up, "fsdp", axis=0, tiled=True),
        lax.all_gather(shared_down, "fsdp", axis=0, tiled=True),
    )
    gain_two = gain_two.astype(jnp.float32)
    normed_two = rms_norm(mixed, gain_two).astype(jnp.bfloat16)
    logits = matmul(normed_two, router_mat)
    expert_count = logits.shape[1]
    expert_ids = jnp.arange(expert_count, dtype=jnp.int32)
    picks = route_ids[:, :, None] == expert_ids[None, None, :]
    chosen = jnp.sum(jnp.where(picks, logits[:, None, :], 0.0), axis=-1)
    gates = jax.nn.softmax(chosen, axis=-1)
    share_gate_in = matmul(normed_two, share_gate_mat)
    share_up_in = matmul(normed_two, share_up_mat)
    share_sig = jax.nn.sigmoid(share_gate_in)
    share_act = (share_gate_in * share_sig * share_up_in).astype(jnp.bfloat16)
    share_out = matmul(share_act, share_down_mat)
    capacity = 5 * rows_dev * top_count // (4 * expert_count)
    flat_ids = route_ids.reshape(-1)
    hits = (flat_ids[:, None] == expert_ids[None, :]).astype(jnp.int32)
    ranks = jnp.sum((jnp.cumsum(hits, axis=0) - hits) * hits, axis=1)
    slots = flat_ids * capacity + ranks
    pair_rows = jnp.arange(rows_dev * top_count, dtype=jnp.int32)
    owner = (
        jnp.full((expert_count * capacity,), rows_dev, jnp.int32)
        .at[slots]
        .set(pair_rows // top_count)
    )
    padded = jnp.concatenate([normed_two, jnp.zeros((1, D), jnp.bfloat16)], axis=0)
    send_rows = jnp.take(padded, owner, axis=0)
    payload = jnp.broadcast_to(send_rows[None], (rep_count, expert_count * capacity, D)).reshape(
        rep_count * expert_count, capacity, D
    )
    own_gate = expert_gate[0]
    own_up = expert_up[0]
    own_down = expert_down[0]
    arrived = lax.all_to_all(
        payload, ("replica", "fsdp", "ctx"), split_axis=0, concat_axis=0, tiled=True
    )
    source_count, item_count, _ = arrived.shape
    flat_rows = arrived.reshape(source_count * item_count, D)
    gate_in = matmul(flat_rows, own_gate)
    up_in = matmul(flat_rows, own_up)
    act_rows = (gate_in * jax.nn.sigmoid(gate_in) * up_in).astype(jnp.bfloat16)
    partial_out = (
        matmul(act_rows, own_down).astype(jnp.bfloat16).reshape(source_count, item_count, D)
    )
    returned = lax.all_to_all(
        partial_out, ("replica", "fsdp", "ctx"), split_axis=0, concat_axis=0, tiled=True
    )
    returned, received = (returned, arrived)
    slot_out = jnp.sum(
        returned.astype(jnp.float32).reshape(rep_count, expert_count * capacity, D), axis=0
    )
    picked = jnp.take(slot_out, slots, axis=0).reshape(rows_dev, top_count, D)
    final = mixed + share_out + jnp.sum(gates[:, :, None] * picked, axis=1)
    error_rows = final - target
    error_total = total(
        jnp.sum(
            (valid_rows[:, None] * error_rows * error_rows).reshape(rows_dev, D // 128, 128),
            axis=(0, 1),
        )[None]
    )
    loss_value = error_total / (valid_count * D)
    grad_final = 2.0 / (valid_count * D) * valid_rows[:, None] * error_rows
    grad_gate = jnp.sum(picked * grad_final[:, None, :], axis=-1)
    grad_chosen = gates * (grad_gate - jnp.sum(gates * grad_gate, axis=-1, keepdims=True))
    grad_logits = jnp.sum(jnp.where(picks, grad_chosen[:, :, None], 0.0), axis=1).astype(
        jnp.bfloat16
    )
    row_grads = (gates[:, :, None] * grad_final[:, None, :]).reshape(rows_dev * top_count, D)
    slot_source = (
        jnp.full((expert_count * capacity,), rows_dev * top_count, jnp.int32)
        .at[slots]
        .set(pair_rows)
    )
    slot_grads = jnp.take(
        jnp.concatenate([row_grads, jnp.zeros((1, D), jnp.float32)], axis=0), slot_source, axis=0
    ).astype(jnp.bfloat16)
    grad_payload = jnp.broadcast_to(
        slot_grads[None], (rep_count, expert_count * capacity, D)
    ).reshape(rep_count * expert_count, capacity, D)
    grad_in = lax.all_to_all(
        grad_payload, ("replica", "fsdp", "ctx"), split_axis=0, concat_axis=0, tiled=True
    )
    rows_flat = received.reshape(-1, D)
    grads_flat = grad_in.reshape(-1, D)
    gate_again = matmul(rows_flat, own_gate)
    up_again = matmul(rows_flat, own_up)
    sigmoid_again = jax.nn.sigmoid(gate_again)
    silu_again = gate_again * sigmoid_again
    act_again = (silu_again * up_again).astype(jnp.bfloat16)
    expert_down_grad = rows_dot(act_again, grads_flat)
    grad_act = cols_dot(grads_flat, own_down)
    grad_gate_in = (grad_act * up_again * silu_slope(gate_again, sigmoid_again)).astype(
        jnp.bfloat16
    )
    grad_up_in = (grad_act * silu_again).astype(jnp.bfloat16)
    expert_gate_grad = rows_dot(rows_flat, grad_gate_in)
    expert_up_grad = rows_dot(rows_flat, grad_up_in)
    grad_rows = (
        (cols_dot(grad_gate_in, own_gate) + cols_dot(grad_up_in, own_up))
        .astype(jnp.bfloat16)
        .reshape(received.shape)
    )
    grad_back = lax.all_to_all(
        grad_rows, ("replica", "fsdp", "ctx"), split_axis=0, concat_axis=0, tiled=True
    )
    grad_slots = jnp.sum(
        grad_back.astype(jnp.float32).reshape(rep_count, expert_count * capacity, D), axis=0
    )
    grad_normed_two = jnp.sum(
        jnp.take(grad_slots, slots, axis=0).reshape(rows_dev, top_count, D), axis=1
    )
    grad_shared = grad_final.astype(jnp.bfloat16)
    g_share_down = sum_rows(
        rows_dot(own_columns(share_act), gather_tokens(grad_shared))
    )
    grad_share_act = cols_dot(grad_shared, share_down_mat)
    grad_share_gate = (grad_share_act * share_up_in * silu_slope(share_gate_in, share_sig)).astype(
        jnp.bfloat16
    )
    grad_share_up = (grad_share_act * share_gate_in * share_sig).astype(jnp.bfloat16)
    normed_two_own = own_columns(normed_two)
    share_width = grad_share_gate.shape[1]
    g_share_both = sum_rows(
        rows_dot(
            normed_two_own,
            gather_tokens(jnp.concatenate([grad_share_gate, grad_share_up], axis=1)),
        )
    )
    g_share_gate, g_share_up = g_share_both[:, :share_width], g_share_both[:, share_width:]
    full_router = rows_dot(normed_two, grad_logits)
    grad_normed_two = (
        grad_normed_two
        + cols_dot(grad_share_gate, share_gate_mat)
        + cols_dot(grad_share_up, share_up_mat)
        + cols_dot(grad_logits, router_mat)
    )
    _, norm_two_back = jax.vjp(rms_norm, mixed, gain_two)
    grad_mixed_norm, gain_two_grad = norm_two_back(grad_normed_two)
    grad_mixed = grad_final + grad_mixed_norm
    grad_mix = grad_mixed.astype(jnp.bfloat16)
    g_out = sum_rows(rows_dot(own_columns(attended), gather_tokens(grad_mix)))
    grad_att = cols_dot(grad_mix, out_mat).astype(jnp.bfloat16).reshape(rows_dev, HEADS, VDIM)
    scores = score_rows()
    prob_rows = jnp.exp(scores - log_total)
    prob_low = prob_rows.astype(jnp.bfloat16)
    grad_value = jnp.einsum("hqk,qhv->khv", prob_low, grad_att, preferred_element_type=jnp.float32)
    grad_probs = jnp.einsum(
        "qhv,khv->hqk", grad_att, value_rows, preferred_element_type=jnp.float32
    )
    row_dot = jnp.sum(prob_rows * grad_probs, axis=-1, keepdims=True)
    grad_scores = (prob_rows * (grad_probs - row_dot)).astype(jnp.bfloat16)
    grad_query = (
        jnp.einsum("hqk,khd->qhd", grad_scores, key_full, preferred_element_type=jnp.float32)
        * score_scale
    )
    grad_key = (
        jnp.einsum("hqk,qhd->khd", grad_scores, query_rot, preferred_element_type=jnp.float32)
        * score_scale
    )
    grad_expanded = (
        jnp.concatenate([grad_key[..., :NOPE], grad_value], axis=-1)
        .astype(jnp.bfloat16)
        .reshape(key_count, HEADS * (NOPE + VDIM))
    )
    full_expand = rows_dot(latent_all, grad_expanded)
    grad_latent_all = cols_dot(grad_expanded, expand_mat)
    grad_rope_all = jnp.sum(grad_key[..., NOPE:], axis=1)
    grad_latent_rope = lax.psum_scatter(
        jnp.concatenate([grad_latent_all, grad_rope_all], axis=1).astype(jnp.bfloat16),
        "ctx",
        scatter_dimension=0,
        tiled=True,
    ).astype(jnp.float32)
    grad_latent_own, grad_rope_own = grad_latent_rope[:, :LATENT], grad_latent_rope[:, LATENT:]
    _, latent_back = jax.vjp(rms_norm, latent_part, gain_latent)
    grad_latent_part, gain_latent_grad = latent_back(grad_latent_own)
    _, rope_back = jax.vjp(turn_key, rope_part)
    (grad_rope_raw,) = rope_back(grad_rope_own)
    grad_latent_raw = jnp.concatenate([grad_latent_part, grad_rope_raw], axis=-1).astype(
        jnp.bfloat16
    )
    _, query_back = jax.vjp(turn_query, query_raw[..., NOPE:])
    (grad_query_rope,) = query_back(grad_query[..., NOPE:])
    grad_query_raw = (
        jnp.concatenate([grad_query[..., :NOPE], grad_query_rope], axis=-1)
        .astype(jnp.bfloat16)
        .reshape(rows_dev, HEADS * (NOPE + ROPE))
    )
    query_width = grad_query_raw.shape[1]
    own_first = rows_dot(
        own_columns(normed),
        gather_tokens(jnp.concatenate([grad_query_raw, grad_latent_raw], axis=1)),
    )
    grad_normed = cols_dot(grad_query_raw, query_mat) + cols_dot(grad_latent_raw, latent_mat)
    _, norm_one_back = jax.vjp(rms_norm, resid, gain_one)
    grad_resid_norm, gain_one_grad = norm_one_back(grad_normed)
    input_grad = grad_mixed + grad_resid_norm
    fsdp_count = lax.axis_size("fsdp")
    own_expand = scatter_rows(full_expand, "fsdp")
    own_expand_rows = own_expand.shape[0]
    pieces = own_first.shape[0] // own_expand_rows
    expand_width = own_expand.shape[1] // pieces
    own_expand = jnp.concatenate(
        [own_expand[:, i * expand_width : (i + 1) * expand_width] for i in range(pieces)], axis=0
    )
    latent_column = jnp.concatenate(
        [
            gain_latent_grad.reshape(fsdp_count, own_expand_rows),
            jnp.zeros((fsdp_count, (D - LATENT) // fsdp_count), jnp.float32),
        ],
        axis=1,
    ).reshape(D, 1)
    small = scatter_rows(
        jnp.concatenate(
            [full_router, gain_one_grad[:, None], gain_two_grad[:, None], latent_column], axis=1
        ),
        "fsdp",
    )
    last = sum_rows(jnp.concatenate([own_first, own_expand, small], axis=1))
    g_query, g_latent = last[:, :query_width], last[:, query_width : own_first.shape[1]]
    start = own_first.shape[1]
    g_expand = jnp.concatenate(
        [
            last[i * own_expand_rows : (i + 1) * own_expand_rows, start : start + expand_width]
            for i in range(pieces)
        ],
        axis=1,
    )
    start += expand_width
    g_router = last[:, start : start + expert_count]
    start += expert_count
    g_gain_one = last[:, start]
    g_gain_two = last[:, start + 1]
    g_gain_latent = last[:own_expand_rows, start + 2]
    return (
        final.astype(jnp.bfloat16).reshape(1, rows_dev, D),
        loss_value,
        input_grad.reshape(1, rows_dev, D),
        g_gain_one,
        g_query,
        g_latent,
        g_gain_latent,
        g_expand,
        g_out,
        g_gain_two,
        g_router,
        g_share_gate,
        g_share_up,
        g_share_down,
        expert_gate_grad[None],
        expert_up_grad[None],
        expert_down_grad[None],
    )


def solution(mesh):
    return jax.shard_map(
        per_device,
        mesh=mesh,
        in_specs=(
            P(("replica", "fsdp"), "ctx", None),
            P(("replica", "fsdp"), "ctx", None),
            P(("replica", "fsdp"), "ctx"),
            P(("replica", "fsdp"), None),
            P(("replica", "fsdp"), "ctx", None),
            P("fsdp"),
            P("fsdp", None),
            P("fsdp", None),
            P("fsdp"),
            P("fsdp", None),
            P("fsdp", None),
            P("fsdp"),
            P("fsdp", None),
            P("fsdp", None),
            P("fsdp", None),
            P("fsdp", None),
            P(("fsdp", "ctx"), None, "replica"),
            P(("fsdp", "ctx"), None, "replica"),
            P(("fsdp", "ctx"), "replica", None),
        ),
        out_specs=(
            P(("replica", "fsdp"), "ctx", None),
            P(),
            P(("replica", "fsdp"), "ctx", None),
            P("fsdp"),
            P("fsdp", None),
            P("fsdp", None),
            P("fsdp"),
            P("fsdp", None),
            P("fsdp", None),
            P("fsdp"),
            P("fsdp", None),
            P("fsdp", None),
            P("fsdp", None),
            P("fsdp", None),
            P(("fsdp", "ctx"), None, "replica"),
            P(("fsdp", "ctx"), None, "replica"),
            P(("fsdp", "ctx"), "replica", None),
        ),
        check_vma=False,
    )
```

```python
import functools

import jax
import jax.numpy as jnp
from jax import lax
from jax.experimental import pallas as pl
from jax.experimental.pallas import tpu as pltpu
from jax.sharding import PartitionSpec as P

D = 2048
HEADS = 16
NOPE = 128
ROPE = 64
VDIM = 128
LATENT = 512


def rms_norm(values, gain_vec):
    return values * lax.rsqrt(jnp.mean(values * values, axis=-1, keepdims=True) + 1e-06) * gain_vec


def rotate(values, cosine, sine_part):
    half_width = values.shape[-1] // 2
    first_half = values[..., :half_width]
    second = values[..., half_width:]
    return jnp.concatenate(
        [first_half * cosine - second * sine_part, first_half * sine_part + second * cosine],
        axis=-1,
    )


def rows_dot(first_mat, second_mat):
    return lax.dot_general(
        first_mat, second_mat, (((0,), (0,)), ((), ())), preferred_element_type=jnp.float32
    )


def cols_dot(first_mat, second_mat):
    return lax.dot_general(
        first_mat, second_mat, (((1,), (1,)), ((), ())), preferred_element_type=jnp.float32
    )


def matmul(first_mat, second_mat):
    return jnp.dot(first_mat, second_mat, preferred_element_type=jnp.float32)


def silu_slope(gate_in, sigmoid_in):
    return sigmoid_in * (1.0 + gate_in * (1.0 - sigmoid_in))


def masks(count):
    found = []
    mask = count // 2
    while mask:
        found.append(mask)
        mask //= 2
    return found


def swap(values, axis, mask):
    count = lax.axis_size(axis)
    return lax.ppermute(values, axis, [(i, i ^ mask) for i in range(count)])


def upper(axis, mask):
    return (lax.axis_index(axis) // mask) % 2 == 1


def halves(values, axis, mask, dim):
    size = values.shape[dim] // 2
    low = lax.slice_in_dim(values, 0, size, axis=dim)
    high = lax.slice_in_dim(values, size, 2 * size, axis=dim)
    up = upper(axis, mask)
    return jnp.where(up, low, high), jnp.where(up, high, low)


def join_halves(mine, other, axis, mask):
    up = upper(axis, mask)
    return jnp.concatenate([jnp.where(up, other, mine), jnp.where(up, mine, other)], axis=0)


def gather_tokens(values):
    for mask in masks(lax.axis_size("fsdp")):
        values = jnp.concatenate([values, swap(values, "fsdp", mask)], axis=0)
    return values


def own_columns(values):
    for mask in masks(lax.axis_size("fsdp")):
        send, keep = halves(values, "fsdp", mask, 1)
        values = jnp.concatenate([keep, swap(send, "fsdp", mask)], axis=0)
    return values


def scatter_rows(values, axis):
    for mask in masks(lax.axis_size(axis)):
        send, keep = halves(values, axis, mask, 0)
        values = keep + swap(send.astype(jnp.bfloat16), axis, mask).astype(jnp.float32)
    return values


def sum_rows(values):
    values = scatter_rows(values, "replica")
    ctx_masks = masks(lax.axis_size("ctx"))[::-1]
    for mask in ctx_masks:
        send, keep = halves(values, "ctx", mask, 0)
        values = keep + swap(send.astype(jnp.bfloat16), "ctx", mask).astype(jnp.float32)
    values = values.astype(jnp.bfloat16)
    for mask in ctx_masks[::-1]:
        values = join_halves(values, swap(values, "ctx", mask), "ctx", mask)
    for mask in masks(lax.axis_size("replica"))[::-1]:
        values = join_halves(values, swap(values, "replica", mask), "replica", mask)
    return values.astype(jnp.float32)


def total(value):
    spread = jnp.full((8, 128), value, jnp.float32)
    for axis in ("fsdp", "replica", "ctx"):
        for mask in masks(lax.axis_size(axis)):
            spread = spread + swap(spread, axis, mask)
    return spread[0, 0]


def column_dot(first_mat, second_mat):
    return lax.dot_general(
        first_mat, second_mat, (((0,), (0,)), ((), ())), preferred_element_type=jnp.float32
    )


def turned_query(q_ref, cos_ref, sin_ref, head):
    start = head * (NOPE + ROPE)
    flat = q_ref[:, start : start + NOPE].astype(jnp.bfloat16)
    first = q_ref[:, start + NOPE : start + NOPE + ROPE // 2]
    second = q_ref[:, start + NOPE + ROPE // 2 : start + NOPE + ROPE]
    cosine, sine_part = cos_ref[...], sin_ref[...]
    turned = jnp.concatenate(
        [first * cosine - second * sine_part, first * sine_part + second * cosine], axis=1
    ).astype(jnp.bfloat16)
    return flat, turned


PAIR = 2


def attention_kernel(q_ref, e_ref, rope_ref, cos_ref, sin_ref, kb_ref, qb_ref, out_ref):
    allowed = kb_ref[...] <= qb_ref[...]
    for head in range(PAIR):
        flat, turned = turned_query(q_ref, cos_ref, sin_ref, head)
        at = head * (NOPE + VDIM)
        scores = (
            cols_dot(flat, e_ref[:, at : at + NOPE]) + cols_dot(turned, rope_ref[...])
        ) * (NOPE + ROPE) ** (-0.5)
        scores = jnp.where(allowed, scores, -1e30)
        weights = jnp.exp(scores - jnp.max(scores, axis=1, keepdims=True))
        probs = weights * (1.0 / jnp.sum(weights, axis=1, keepdims=True))
        out_ref[:, head * VDIM : (head + 1) * VDIM] = matmul(
            probs.astype(jnp.bfloat16), e_ref[:, at + NOPE : at + NOPE + VDIM]
        ).astype(jnp.bfloat16)


def attention_back_kernel(
    q_ref, e_ref, rope_ref, cos_ref, sin_ref, kb_ref, qb_ref, ga_ref, gq_ref, ge_ref, gr_ref
):
    @pl.when(pl.program_id(0) == 0)
    def _():
        gr_ref[...] = jnp.zeros_like(gr_ref)

    allowed = kb_ref[...] <= qb_ref[...]
    scale = (NOPE + ROPE) ** (-0.5)
    cosine, sine_part = cos_ref[...], sin_ref[...]
    for head in range(PAIR):
        flat, turned = turned_query(q_ref, cos_ref, sin_ref, head)
        at = head * (NOPE + VDIM)
        key_flat, value = e_ref[:, at : at + NOPE], e_ref[:, at + NOPE : at + NOPE + VDIM]
        grad_att = ga_ref[:, head * VDIM : (head + 1) * VDIM]
        scores = (cols_dot(key_flat, flat) + cols_dot(rope_ref[...], turned)) * scale
        scores = jnp.where(allowed, scores, -1e30)
        weights = jnp.exp(scores - jnp.max(scores, axis=0, keepdims=True))
        probs = weights * (1.0 / jnp.sum(weights, axis=0, keepdims=True))
        grad_value = matmul(probs.astype(jnp.bfloat16), grad_att)
        grad_probs = cols_dot(value, grad_att)
        row_dot = jnp.sum(probs * grad_probs, axis=0, keepdims=True)
        grad_scores = (probs * (grad_probs - row_dot)).astype(jnp.bfloat16)
        ge_ref[:, at : at + NOPE] = (matmul(grad_scores, flat) * scale).astype(jnp.bfloat16)
        ge_ref[:, at + NOPE : at + NOPE + VDIM] = grad_value.astype(jnp.bfloat16)
        gr_ref[...] += matmul(grad_scores, turned) * scale
        grad_flat = column_dot(grad_scores, key_flat) * scale
        grad_turned = column_dot(grad_scores, rope_ref[...]) * scale
        first, second = grad_turned[:, : ROPE // 2], grad_turned[:, ROPE // 2 :]
        start = head * (NOPE + ROPE)
        gq_ref[:, start : start + NOPE + ROPE] = jnp.concatenate(
            [
                grad_flat,
                first * cosine + second * sine_part,
                second * cosine - first * sine_part,
            ],
            axis=1,
        ).astype(jnp.bfloat16)


def whole(shape):
    return pl.BlockSpec(shape, lambda i: (0, 0))


def attention(query_raw, expanded, rope_all, cosine, sine_part, key_block, query_block):
    rows, keys = query_raw.shape[0], expanded.shape[0]
    return pl.pallas_call(
        attention_kernel,
        grid=(HEADS // PAIR,),
        in_specs=[
            pl.BlockSpec((rows, PAIR * (NOPE + ROPE)), lambda i: (0, i)),
            pl.BlockSpec((keys, PAIR * (NOPE + VDIM)), lambda i: (0, i)),
            whole((keys, ROPE)),
            whole((rows, ROPE // 2)),
            whole((rows, ROPE // 2)),
            whole((1, keys)),
            whole((rows, 1)),
        ],
        out_specs=pl.BlockSpec((rows, PAIR * VDIM), lambda i: (0, i)),
        out_shape=jax.ShapeDtypeStruct((rows, HEADS * VDIM), jnp.bfloat16),
        compiler_params=pltpu.CompilerParams(vmem_limit_bytes=40 * 1024 * 1024),
        cost_estimate=pl.CostEstimate(
            flops=2 * rows * keys * HEADS * (NOPE + ROPE + VDIM),
            bytes_accessed=12 * 1024 * 1024,
            transcendentals=rows * keys * HEADS,
        ),
        name="attention",
    )(
        query_raw,
        expanded,
        rope_all,
        cosine,
        sine_part,
        key_block.reshape(1, keys),
        query_block.reshape(rows, 1),
    )


def attention_back(
    query_raw, expanded, rope_all, cosine, sine_part, key_block, query_block, grad_att
):
    rows, keys = query_raw.shape[0], expanded.shape[0]
    return pl.pallas_call(
        attention_back_kernel,
        grid=(HEADS // PAIR,),
        in_specs=[
            pl.BlockSpec((rows, PAIR * (NOPE + ROPE)), lambda i: (0, i)),
            pl.BlockSpec((keys, PAIR * (NOPE + VDIM)), lambda i: (0, i)),
            whole((keys, ROPE)),
            whole((rows, ROPE // 2)),
            whole((rows, ROPE // 2)),
            whole((keys, 1)),
            whole((1, rows)),
            pl.BlockSpec((rows, PAIR * VDIM), lambda i: (0, i)),
        ],
        out_specs=(
            pl.BlockSpec((rows, PAIR * (NOPE + ROPE)), lambda i: (0, i)),
            pl.BlockSpec((keys, PAIR * (NOPE + VDIM)), lambda i: (0, i)),
            whole((keys, ROPE)),
        ),
        out_shape=(
            jax.ShapeDtypeStruct((rows, HEADS * (NOPE + ROPE)), jnp.bfloat16),
            jax.ShapeDtypeStruct((keys, HEADS * (NOPE + VDIM)), jnp.bfloat16),
            jax.ShapeDtypeStruct((keys, ROPE), jnp.float32),
        ),
        compiler_params=pltpu.CompilerParams(vmem_limit_bytes=40 * 1024 * 1024),
        cost_estimate=pl.CostEstimate(
            flops=2 * rows * keys * HEADS * (3 * (NOPE + ROPE) + 2 * VDIM),
            bytes_accessed=24 * 1024 * 1024,
            transcendentals=rows * keys * HEADS,
        ),
        name="attention_back",
    )(
        query_raw,
        expanded,
        rope_all,
        cosine,
        sine_part,
        key_block.reshape(keys, 1),
        query_block.reshape(1, rows),
        grad_att,
    )


MESH = pl.DeviceIdType.MESH
STEP = 8


def rows_of(ref, first, count):
    block = ref[pl.ds(first, count)].astype(jnp.float32)
    return block.reshape(count * block.shape[1], block.shape[2]).astype(jnp.bfloat16)


def put_rows(ref, first, count, rows):
    ref[pl.ds(first, count)] = rows.reshape(count, ref.shape[1], ref.shape[2]).astype(ref.dtype)


def exchange(send, arrived, part, back, xin, ret, sems, group, prepare):
    n, step = send.shape[0], STEP
    local_sem, ssem, rsem, fsem, gsem, psem, qsem, bsem, tsem = sems
    columns = lax.axis_size("ctx")
    me = lax.axis_index("fsdp") * columns + lax.axis_index("ctx")
    other = {"replica": 1 - lax.axis_index("replica")}

    def place(index):
        return {"fsdp": index // columns, "ctx": index % columns}

    def dispatch(slot):
        to = (me + slot) % n
        return pltpu.make_async_remote_copy(
            src_ref=send.at[to],
            dst_ref=arrived.at[slot],
            send_sem=ssem.at[slot],
            recv_sem=rsem.at[slot],
            device_id=place(to),
            device_id_type=MESH,
        )

    def forward(slot):
        return pltpu.make_async_remote_copy(
            src_ref=arrived.at[slot],
            dst_ref=arrived.at[n + slot],
            send_sem=fsem.at[slot],
            recv_sem=gsem.at[slot],
            device_id=other,
            device_id_type=MESH,
        )

    def across(slot):
        return pltpu.make_async_remote_copy(
            src_ref=part.at[n + slot],
            dst_ref=xin.at[slot],
            send_sem=psem.at[slot],
            recv_sem=qsem.at[slot],
            device_id=other,
            device_id_type=MESH,
        )

    def give_back(slot, from_index):
        return pltpu.make_async_remote_copy(
            src_ref=back.at[slot],
            dst_ref=ret.at[from_index],
            send_sem=bsem.at[slot],
            recv_sem=tsem.at[slot],
            device_id=place((me + n - slot) % n),
            device_id_type=MESH,
        )

    barrier = pltpu.get_barrier_semaphore()

    @pl.loop(1, n)
    def _(slot):
        pl.semaphore_signal(
            barrier, inc=1, device_id=place((me + slot) % n), device_id_type=MESH
        )

    pl.semaphore_signal(barrier, inc=1, device_id=other, device_id_type=MESH)
    pl.semaphore_wait(barrier, n)

    own = pltpu.make_async_copy(send.at[me], arrived.at[0], local_sem.at[0])
    own.start()

    @pl.loop(1, n)
    def _(slot):
        dispatch(slot).start()

    own.wait()
    forward(0).start()
    prepare()

    @pl.loop(0, n // step)
    def _(turn):
        @pl.loop(0, step)
        def _(i):
            slot = turn * step + i

            @pl.when(slot > 0)
            def _():
                dispatch(slot).wait_recv()
                forward(slot).start()

        group(turn * step)

    @pl.loop(0, n // step)
    def _(turn):
        @pl.loop(0, step)
        def _(i):
            forward(turn * step + i).wait_recv()

        group(n + turn * step)

        @pl.loop(0, step)
        def _(i):
            across(turn * step + i).start()

    @pl.loop(0, n)
    def _(slot):
        across(slot).wait_recv()
        back[pl.ds(slot, 1)] = (
            part[pl.ds(slot, 1)].astype(jnp.float32) + xin[pl.ds(slot, 1)].astype(jnp.float32)
        ).astype(jnp.bfloat16)

        @pl.when(slot > 0)
        def _():
            give_back(slot, me).start()

    keep = pltpu.make_async_copy(back.at[0], ret.at[me], local_sem.at[0])
    keep.start()
    keep.wait()

    @pl.loop(1, n)
    def _(slot):
        dispatch(slot).wait_send()
        give_back(slot, (me + slot) % n).wait()

    @pl.loop(0, n)
    def _(slot):
        forward(slot).wait_send()
        across(slot).wait_send()


def experts_kernel(
    send, gate, up, down, kept, ret, w_gate, w_up, w_down, arrived, part, back, xin, wsem, *sems
):
    n = send.shape[0]
    loads = [
        pltpu.make_async_copy(source, target, wsem.at[i])
        for i, (source, target) in enumerate(((gate, w_gate), (up, w_up), (down, w_down)))
    ]

    def prepare():
        for load in loads:
            load.wait()

    def group(first):
        rows = rows_of(arrived, first, STEP)
        gate_in = matmul(rows, w_gate[...])
        act = (gate_in * jax.nn.sigmoid(gate_in) * matmul(rows, w_up[...])).astype(jnp.bfloat16)
        put_rows(part, first, STEP, matmul(act, w_down[...]))

    for load in loads:
        load.start()
    exchange(send, arrived, part, back, xin, ret, sems, group, prepare)
    save = pltpu.make_async_copy(arrived, kept, wsem.at[0])
    save.start()
    save.wait()


def experts_back_kernel(
    send,
    rows_in,
    gate,
    up,
    down,
    kept,
    act_out,
    gg_out,
    gu_out,
    ret,
    w_gate,
    w_up,
    w_down,
    rows_kept,
    slope,
    silu,
    arrived,
    part,
    back,
    xin,
    wsem,
    *sems,
):
    n = send.shape[0]
    loads = [
        pltpu.make_async_copy(source, target, wsem.at[i])
        for i, (source, target) in enumerate(
            ((rows_in, rows_kept), (gate, w_gate), (up, w_up), (down, w_down))
        )
    ]
    size = STEP * send.shape[1]

    def prepare():
        for load in loads:
            load.wait()

        @pl.loop(0, 2 * n // STEP)
        def _(turn):
            rows = rows_of(rows_kept, turn * STEP, STEP)
            at = pl.ds(pl.multiple_of(turn * size, size), size)
            gate_in = matmul(rows, w_gate[...])
            up_in = matmul(rows, w_up[...])
            sigmoid = jax.nn.sigmoid(gate_in)
            silu_in = gate_in * sigmoid
            silu[at] = silu_in
            slope[at] = up_in * silu_slope(gate_in, sigmoid)
            act_out[at] = (silu_in * up_in).astype(jnp.bfloat16)

    def group(first):
        grads = rows_of(arrived, first, STEP)
        at = pl.ds(pl.multiple_of(first * send.shape[1], size), size)
        grad_act = cols_dot(grads, w_down[...])
        grad_gate_in = (grad_act * slope[at]).astype(jnp.bfloat16)
        grad_up_in = (grad_act * silu[at]).astype(jnp.bfloat16)
        gg_out[at] = grad_gate_in
        gu_out[at] = grad_up_in
        put_rows(
            part,
            first,
            STEP,
            cols_dot(grad_gate_in, w_gate[...]) + cols_dot(grad_up_in, w_up[...]),
        )

    for load in loads:
        load.start()
    exchange(send, arrived, part, back, xin, ret, sems, group, prepare)
    save = pltpu.make_async_copy(arrived, kept, wsem.at[0])
    save.start()
    save.wait()


def exchange_scratch(n, cap, width):
    return [
        pltpu.VMEM((2 * n, cap, width), jnp.bfloat16),
        pltpu.VMEM((2 * n, cap, width), jnp.bfloat16),
        pltpu.VMEM((n, cap, width), jnp.bfloat16),
        pltpu.VMEM((n, cap, width), jnp.bfloat16),
        pltpu.SemaphoreType.DMA((4,)),
        pltpu.SemaphoreType.DMA((1,)),
    ] + [pltpu.SemaphoreType.DMA((n,)) for _ in range(8)]


def any_spec():
    return pl.BlockSpec(memory_space=pl.ANY)


def experts(send, gate, up, down):
    n, cap, width = send.shape
    hidden = gate.shape[1]
    return pl.pallas_call(
        experts_kernel,
        in_specs=[any_spec()] * 4,
        out_specs=(any_spec(), any_spec()),
        out_shape=(
            jax.ShapeDtypeStruct((2 * n, cap, width), jnp.bfloat16),
            jax.ShapeDtypeStruct((n, cap, width), jnp.bfloat16),
        ),
        scratch_shapes=[
            pltpu.VMEM((width, hidden), jnp.bfloat16),
            pltpu.VMEM((width, hidden), jnp.bfloat16),
            pltpu.VMEM((hidden, width), jnp.bfloat16),
        ]
        + exchange_scratch(n, cap, width),
        compiler_params=pltpu.CompilerParams(
            collective_id=0, has_side_effects=True, vmem_limit_bytes=60 * 1024 * 1024
        ),
        cost_estimate=pl.CostEstimate(
            flops=2 * 2 * n * cap * width * hidden * 3,
            bytes_accessed=400 * 1024 * 1024,
            transcendentals=2 * n * cap * hidden,
        ),
        name="experts",
    )(send, gate, up, down)


def experts_back(send, rows, gate, up, down):
    n, cap, width = send.shape
    hidden = gate.shape[1]
    vmem = pl.BlockSpec(memory_space=pltpu.VMEM)
    hidden_rows = jax.ShapeDtypeStruct((2 * n * cap, hidden), jnp.bfloat16)
    return pl.pallas_call(
        experts_back_kernel,
        in_specs=[any_spec()] * 5,
        out_specs=(any_spec(), vmem, vmem, vmem, any_spec()),
        out_shape=(
            jax.ShapeDtypeStruct((2 * n, cap, width), jnp.bfloat16),
            hidden_rows,
            hidden_rows,
            hidden_rows,
            jax.ShapeDtypeStruct((n, cap, width), jnp.bfloat16),
        ),
        scratch_shapes=[
            pltpu.VMEM((width, hidden), jnp.bfloat16),
            pltpu.VMEM((width, hidden), jnp.bfloat16),
            pltpu.VMEM((hidden, width), jnp.bfloat16),
            pltpu.VMEM((2 * n, cap, width), jnp.bfloat16),
            pltpu.VMEM((2 * n * cap, hidden), jnp.float32),
            pltpu.VMEM((2 * n * cap, hidden), jnp.float32),
        ]
        + exchange_scratch(n, cap, width),
        compiler_params=pltpu.CompilerParams(
            collective_id=1, has_side_effects=True, vmem_limit_bytes=63 * 1024 * 1024
        ),
        cost_estimate=pl.CostEstimate(
            flops=2 * 2 * n * cap * width * hidden * 5,
            bytes_accessed=400 * 1024 * 1024,
            transcendentals=2 * n * cap * hidden,
        ),
        name="experts_back",
    )(send, rows, gate, up, down)


def per_device(
    hidden_in,
    teacher,
    valid_mask,
    layout,
    routes,
    attn_gain,
    w_query,
    w_latent,
    latent_gain,
    w_expand,
    w_out,
    ffn_gain,
    w_router,
    shared_gate,
    shared_up,
    shared_down,
    expert_gate,
    expert_up,
    expert_down,
):
    rows_dev = hidden_in.shape[1]
    offset = lax.axis_index("ctx") * rows_dev
    resid = hidden_in.reshape(rows_dev, D).astype(jnp.float32)
    target = teacher.reshape(rows_dev, D).astype(jnp.float32)
    valid_rows = valid_mask.reshape(rows_dev).astype(jnp.float32)
    key_block = layout[0]
    query_block = lax.dynamic_slice_in_dim(key_block, offset, rows_dev)
    route_ids = routes.reshape(rows_dev, routes.shape[-1])
    top_count = route_ids.shape[1]
    fsdp_count = lax.axis_size("fsdp")
    gain_rows, latent_rows = attn_gain.shape[0], latent_gain.shape[0]
    small_all = lax.all_gather(
        jnp.concatenate([attn_gain, ffn_gain, latent_gain, w_router.reshape(-1)])[None],
        "fsdp",
        axis=0,
        tiled=True,
    )
    gain_one = small_all[:, :gain_rows].reshape(D)
    gain_two = small_all[:, gain_rows : 2 * gain_rows].reshape(D)
    gain_latent = small_all[:, 2 * gain_rows : 2 * gain_rows + latent_rows].reshape(LATENT)
    router_mat = small_all[:, 2 * gain_rows + latent_rows :].reshape(D, w_router.shape[1])
    query_mat, latent_mat, expand_mat, out_mat = (
        lax.all_gather(w_query, "fsdp", axis=0, tiled=True),
        lax.all_gather(w_latent, "fsdp", axis=0, tiled=True),
        lax.all_gather(w_expand, "fsdp", axis=0, tiled=True),
        lax.all_gather(w_out, "fsdp", axis=0, tiled=True),
    )
    valid_count = total(jnp.sum(valid_rows))
    gain_one = gain_one.astype(jnp.float32)
    gain_latent = gain_latent.astype(jnp.float32)
    positions = (offset + jnp.arange(rows_dev)).astype(jnp.float32)
    inverse = 10000.0 ** (-jnp.arange(ROPE // 2, dtype=jnp.float32) * (2.0 / ROPE))
    phase = positions[:, None] * inverse[None, :]
    cosine = jnp.cos(phase)
    sine_part = jnp.sin(phase)

    def turn_key(values):
        return rotate(values, cosine, sine_part)

    normed = rms_norm(resid, gain_one).astype(jnp.bfloat16)
    query_raw = matmul(normed, query_mat)
    latent_raw = matmul(normed, latent_mat)
    latent_part = latent_raw[:, :LATENT]
    rope_part = latent_raw[:, LATENT:]
    latent_own = rms_norm(latent_part, gain_latent).astype(jnp.bfloat16)
    rope_own = turn_key(rope_part).astype(jnp.bfloat16)
    latent_rope = lax.all_gather(
        jnp.concatenate([latent_own, rope_own], axis=1), "ctx", axis=0, tiled=True
    )
    latent_all, rope_all = latent_rope[:, :LATENT], latent_rope[:, LATENT:]
    expanded = matmul(latent_all, expand_mat).astype(jnp.bfloat16)
    attended = attention(
        query_raw, expanded, rope_all, cosine, sine_part, key_block, query_block
    )
    mixed = resid + matmul(attended, out_mat)
    share_gate_mat, share_up_mat, share_down_mat = (
        lax.all_gather(shared_gate, "fsdp", axis=0, tiled=True),
        lax.all_gather(shared_up, "fsdp", axis=0, tiled=True),
        lax.all_gather(shared_down, "fsdp", axis=0, tiled=True),
    )
    gain_two = gain_two.astype(jnp.float32)
    normed_two = rms_norm(mixed, gain_two).astype(jnp.bfloat16)
    logits = matmul(normed_two, router_mat)
    expert_count = logits.shape[1]
    expert_ids = jnp.arange(expert_count, dtype=jnp.int32)
    picks = route_ids[:, :, None] == expert_ids[None, None, :]
    chosen = jnp.sum(jnp.where(picks, logits[:, None, :], 0.0), axis=-1)
    gates = jax.nn.softmax(chosen, axis=-1)
    share_gate_in = matmul(normed_two, share_gate_mat)
    share_up_in = matmul(normed_two, share_up_mat)
    share_sig = jax.nn.sigmoid(share_gate_in)
    share_act = (share_gate_in * share_sig * share_up_in).astype(jnp.bfloat16)
    share_out = matmul(share_act, share_down_mat)
    capacity = 5 * rows_dev * top_count // (4 * expert_count)
    capacity = (capacity + 7) // 8 * 8
    flat_ids = route_ids.reshape(-1)
    hits = (flat_ids[:, None] == expert_ids[None, :]).astype(jnp.int32)
    ranks = jnp.sum((jnp.cumsum(hits, axis=0) - hits) * hits, axis=1)
    slots = flat_ids * capacity + ranks
    pair_rows = jnp.arange(rows_dev * top_count, dtype=jnp.int32)
    owner = (
        jnp.full((expert_count * capacity,), rows_dev, jnp.int32)
        .at[slots]
        .set(pair_rows // top_count)
    )
    padded = jnp.concatenate([normed_two, jnp.zeros((1, D), jnp.bfloat16)], axis=0)
    send_rows = jnp.take(padded, owner, axis=0)
    own_gate = expert_gate[0]
    own_up = expert_up[0]
    own_down = expert_down[0]
    received, returned = experts(
        send_rows.reshape(expert_count, capacity, D), own_gate, own_up, own_down
    )
    slot_out = returned.reshape(expert_count * capacity, D).astype(jnp.float32)
    picked = jnp.take(slot_out, slots, axis=0).reshape(rows_dev, top_count, D)
    final = mixed + share_out + jnp.sum(gates[:, :, None] * picked, axis=1)
    error_rows = final - target
    error_total = total(jnp.sum(valid_rows[:, None] * error_rows * error_rows))
    loss_value = error_total / (valid_count * D)
    grad_final = 2.0 / (valid_count * D) * valid_rows[:, None] * error_rows
    grad_gate = jnp.sum(picked * grad_final[:, None, :], axis=-1)
    grad_chosen = gates * (grad_gate - jnp.sum(gates * grad_gate, axis=-1, keepdims=True))
    grad_logits = jnp.sum(jnp.where(picks, grad_chosen[:, :, None], 0.0), axis=1).astype(
        jnp.bfloat16
    )
    row_grads = (gates[:, :, None] * grad_final[:, None, :]).reshape(rows_dev * top_count, D)
    slot_source = (
        jnp.full((expert_count * capacity,), rows_dev * top_count, jnp.int32)
        .at[slots]
        .set(pair_rows)
    )
    slot_grads = jnp.take(
        jnp.concatenate([row_grads, jnp.zeros((1, D), jnp.float32)], axis=0), slot_source, axis=0
    ).astype(jnp.bfloat16)
    grad_in, act_again, grad_gate_in, grad_up_in, grad_back = experts_back(
        slot_grads.reshape(expert_count, capacity, D), received, own_gate, own_up, own_down
    )
    rows_flat = received.reshape(-1, D)
    grads_flat = grad_in.reshape(-1, D)
    expert_down_grad = rows_dot(act_again, grads_flat)
    expert_gate_grad = rows_dot(rows_flat, grad_gate_in)
    expert_up_grad = rows_dot(rows_flat, grad_up_in)
    grad_slots = grad_back.reshape(expert_count * capacity, D).astype(jnp.float32)
    grad_normed_two = jnp.sum(
        jnp.take(grad_slots, slots, axis=0).reshape(rows_dev, top_count, D), axis=1
    )
    grad_shared = grad_final.astype(jnp.bfloat16)
    g_share_down = sum_rows(
        rows_dot(own_columns(share_act), gather_tokens(grad_shared))
    )
    grad_share_act = cols_dot(grad_shared, share_down_mat)
    grad_share_gate = (grad_share_act * share_up_in * silu_slope(share_gate_in, share_sig)).astype(
        jnp.bfloat16
    )
    grad_share_up = (grad_share_act * share_gate_in * share_sig).astype(jnp.bfloat16)
    normed_two_own = own_columns(normed_two)
    share_width = grad_share_gate.shape[1]
    g_share_both = sum_rows(
        rows_dot(
            normed_two_own,
            gather_tokens(jnp.concatenate([grad_share_gate, grad_share_up], axis=1)),
        )
    )
    g_share_gate, g_share_up = g_share_both[:, :share_width], g_share_both[:, share_width:]
    full_router = rows_dot(normed_two, grad_logits)
    grad_normed_two = (
        grad_normed_two
        + cols_dot(grad_share_gate, share_gate_mat)
        + cols_dot(grad_share_up, share_up_mat)
        + cols_dot(grad_logits, router_mat)
    )
    _, norm_two_back = jax.vjp(rms_norm, mixed, gain_two)
    grad_mixed_norm, gain_two_grad = norm_two_back(grad_normed_two)
    grad_mixed = grad_final + grad_mixed_norm
    grad_mix = grad_mixed.astype(jnp.bfloat16)
    g_out = sum_rows(rows_dot(own_columns(attended), gather_tokens(grad_mix)))
    grad_att = cols_dot(grad_mix, out_mat).astype(jnp.bfloat16)
    grad_query_raw, grad_expanded, grad_rope_all = attention_back(
        query_raw, expanded, rope_all, cosine, sine_part, key_block, query_block, grad_att
    )
    full_expand = rows_dot(latent_all, grad_expanded)
    grad_latent_all = cols_dot(grad_expanded, expand_mat)
    grad_latent_rope = lax.psum_scatter(
        jnp.concatenate([grad_latent_all, grad_rope_all], axis=1).astype(jnp.bfloat16),
        "ctx",
        scatter_dimension=0,
        tiled=True,
    ).astype(jnp.float32)
    grad_latent_own, grad_rope_own = grad_latent_rope[:, :LATENT], grad_latent_rope[:, LATENT:]
    _, latent_back = jax.vjp(rms_norm, latent_part, gain_latent)
    grad_latent_part, gain_latent_grad = latent_back(grad_latent_own)
    _, rope_back = jax.vjp(turn_key, rope_part)
    (grad_rope_raw,) = rope_back(grad_rope_own)
    grad_latent_raw = jnp.concatenate([grad_latent_part, grad_rope_raw], axis=-1).astype(
        jnp.bfloat16
    )
    query_width = grad_query_raw.shape[1]
    own_first = rows_dot(
        own_columns(normed),
        gather_tokens(jnp.concatenate([grad_query_raw, grad_latent_raw], axis=1)),
    )
    grad_normed = cols_dot(grad_query_raw, query_mat) + cols_dot(grad_latent_raw, latent_mat)
    _, norm_one_back = jax.vjp(rms_norm, resid, gain_one)
    grad_resid_norm, gain_one_grad = norm_one_back(grad_normed)
    input_grad = grad_mixed + grad_resid_norm
    own_expand = scatter_rows(full_expand, "fsdp")
    own_expand_rows = own_expand.shape[0]
    pieces = own_first.shape[0] // own_expand_rows
    expand_width = own_expand.shape[1] // pieces
    own_expand = jnp.concatenate(
        [own_expand[:, i * expand_width : (i + 1) * expand_width] for i in range(pieces)], axis=0
    )
    latent_column = jnp.concatenate(
        [
            gain_latent_grad.reshape(fsdp_count, own_expand_rows),
            jnp.zeros((fsdp_count, (D - LATENT) // fsdp_count), jnp.float32),
        ],
        axis=1,
    ).reshape(D, 1)
    small = scatter_rows(
        jnp.concatenate(
            [full_router, gain_one_grad[:, None], gain_two_grad[:, None], latent_column], axis=1
        ),
        "fsdp",
    )
    last = sum_rows(jnp.concatenate([own_first, own_expand, small], axis=1))
    g_query, g_latent = last[:, :query_width], last[:, query_width : own_first.shape[1]]
    start = own_first.shape[1]
    g_expand = jnp.concatenate(
        [
            last[i * own_expand_rows : (i + 1) * own_expand_rows, start : start + expand_width]
            for i in range(pieces)
        ],
        axis=1,
    )
    start += expand_width
    g_router = last[:, start : start + expert_count]
    start += expert_count
    g_gain_one = last[:, start]
    g_gain_two = last[:, start + 1]
    g_gain_latent = last[:own_expand_rows, start + 2]
    return (
        final.astype(jnp.bfloat16).reshape(1, rows_dev, D),
        loss_value,
        input_grad.reshape(1, rows_dev, D),
        g_gain_one,
        g_query,
        g_latent,
        g_gain_latent,
        g_expand,
        g_out,
        g_gain_two,
        g_router,
        g_share_gate,
        g_share_up,
        g_share_down,
        expert_gate_grad[None],
        expert_up_grad[None],
        expert_down_grad[None],
    )


def solution(mesh):
    return jax.shard_map(
        per_device,
        mesh=mesh,
        in_specs=(
            P(("replica", "fsdp"), "ctx", None),
            P(("replica", "fsdp"), "ctx", None),
            P(("replica", "fsdp"), "ctx"),
            P(("replica", "fsdp"), None),
            P(("replica", "fsdp"), "ctx", None),
            P("fsdp"),
            P("fsdp", None),
            P("fsdp", None),
            P("fsdp"),
            P("fsdp", None),
            P("fsdp", None),
            P("fsdp"),
            P("fsdp", None),
            P("fsdp", None),
            P("fsdp", None),
            P("fsdp", None),
            P(("fsdp", "ctx"), None, "replica"),
            P(("fsdp", "ctx"), None, "replica"),
            P(("fsdp", "ctx"), "replica", None),
        ),
        out_specs=(
            P(("replica", "fsdp"), "ctx", None),
            P(),
            P(("replica", "fsdp"), "ctx", None),
            P("fsdp"),
            P("fsdp", None),
            P("fsdp", None),
            P("fsdp"),
            P("fsdp", None),
            P("fsdp", None),
            P("fsdp"),
            P("fsdp", None),
            P("fsdp", None),
            P("fsdp", None),
            P("fsdp", None),
            P(("fsdp", "ctx"), None, "replica"),
            P(("fsdp", "ctx"), None, "replica"),
            P(("fsdp", "ctx"), "replica", None),
        ),
        check_vma=False,
    )
```
